512 devices in a mesh: vis: 4 (over y_lo, core), row: 16 (over z), col: 8 (over y_hi, x).
Axes of the slice: x: 4, y: 4 (y_hi: 2, y_lo: 2; y = y_hi * 2 + y_lo), z: 16, core: 2. Of those that a mesh axis runs over, the one named last changes fastest.
Arguments:
- partials: bfloat16 [4, 2, 8192, 8192], P('vis', None, 'row', 'col'), may hold values from -6 to 6
- coverage: int32 [4, 64, 64], P('vis', 'row', 'col'), may hold values from 0 to 1, as said below
- conv_one: float32 [32, 3, 3], replicated, may hold values from -2 to 2
- bias_one: float32 [32], replicated, may hold values from -3 to 3
- conv_two: bfloat16 [3, 3, 32, 32], replicated, may hold values from -0.375 to 0.375
- bias_two: float32 [32], replicated, may hold values from -3 to 3
Outputs:
- features: bfloat16 [32, 4096, 4096], P(None, ('vis', 'row', 'col'))
The draws below stay inside these ranges and needn't reach their ends.
Inputs may be any that keep to these rules, and one draw needn't show every extreme that they name: `coverage`: 0 or 1; blocks near the grid's centre are touched by more groups than those near its corners.
All inputs are finite; a program needn't handle non-finite values.
Results may differ from the reference program's by a relative error of at most 0.014.
Values may be sent and summed in bfloat16 or wider, within the bound.
A program may use at most 64 MiB of HBM per device.

```python
import jax
import jax.numpy as jnp
from jax import lax

BLK = 128
CH = 32
N = 8192
M = 4096
GROUPS = 4
NB = 64


def draw_coverage(key, part):
    offset = jnp.arange(NB, dtype=jnp.int32) * 2 - (NB - 1)
    radius = offset[:, None] * offset[None, :] * 0 + offset[:, None] * offset[:, None] + offset[None, :] * offset[None, :]
    ceiling = 2 * (NB - 1) * (NB - 1) + 1
    picked = jax.random.randint(key, (GROUPS, NB, NB), 0, ceiling)
    return (picked < ceiling - radius * 4 // 5).astype(jnp.int32)


def shard_levels(rng, extent, pieces, smallest, high):
    def one(position, parts):
        draws = jax.random.uniform(jax.random.fold_in(jax.random.fold_in(rng, 6), position), (parts,), jnp.float32, smallest / len(pieces), high / len(pieces))
        return jnp.repeat(jnp.exp(draws), extent[position] // parts).reshape((-1,) + (1,) * (len(extent) - position - 1))

    level = one(*pieces[0])
    for cut in pieces[1:]:
        level = level * one(*cut)
    return level


def scatter_about(key, dims, scale, limit, shards=(), kind=jnp.bfloat16):
    drawn = scale * jax.random.normal(key, dims, jnp.float32)
    if shards:
        drawn = drawn * shard_levels(key, dims, shards, -0.22, 0.18)
    return jnp.clip(drawn, -limit, limit).astype(kind)


def setup_inputs(seed: int = 0) -> dict:
    streams_of = jax.random.split(jax.random.key(seed), 7)
    partials = scatter_about(streams_of[0], (GROUPS, 2, N, N), 1.0, 6.0, ((0, 4), (2, 16), (3, 8)))
    coverage = draw_coverage(jax.random.fold_in(streams_of[6], 71), 0)
    conv_one = scatter_about(streams_of[2], (CH, 3, 3), 9 ** -0.5, 2.0, (), jnp.float32)
    bias_one = scatter_about(streams_of[3], (CH,), 0.5, 3.0, (), jnp.float32)
    conv_two = scatter_about(streams_of[4], (3, 3, CH, CH), (9 * CH) ** -0.5, 0.375)
    bias_two = scatter_about(streams_of[5], (CH,), 0.5, 3.0, (), jnp.float32)
    return {"partials": partials, "coverage": coverage, "conv_one": conv_one, "bias_one": bias_one, "conv_two": conv_two, "bias_two": bias_two}


def reference(partials, coverage, conv_one, bias_one, conv_two, bias_two):
    grid_re = jnp.zeros((N, N), jnp.float32)
    grid_im = jnp.zeros((N, N), jnp.float32)
    for group in range(GROUPS):
        spread = jnp.repeat(jnp.repeat(coverage[group], BLK, axis=0), BLK, axis=1).astype(jnp.float32)
        grid_re = grid_re + spread * partials[group, 0].astype(jnp.float32)
        grid_im = grid_im + spread * partials[group, 1].astype(jnp.float32)
    quarter = jnp.array([1.0, -1.0j, -1.0, 1.0j])
    phase = quarter[jnp.arange(N, dtype=jnp.int32) % 4]
    shifted = (grid_re + 1j * grid_im) * phase[:, None] * phase[None, :]
    spectrum = jnp.fft.ifft2(shifted)[:M, :M] * (N * N)
    signs = (1 - 2 * (jnp.arange(M, dtype=jnp.int32) % 2)).astype(jnp.float32)
    image = jnp.real(spectrum).astype(jnp.float32) * signs[:, None] * signs[None, :] / N
    image = image.T
    first = lax.conv_general_dilated(image[None, None], conv_one[:, None], (1, 1), "SAME",
                                     precision=lax.Precision.HIGHEST)
    hidden = jnp.maximum(first[0] + bias_one[:, None, None], 0.0).astype(jnp.bfloat16)
    kernel = jnp.transpose(conv_two, (2, 3, 0, 1))
    second = lax.conv_general_dilated(hidden[None], kernel, (1, 1), "SAME",
                                      preferred_element_type=jnp.float32)
    return (second[0] + bias_two[:, None, None]).astype(jnp.bfloat16)
```

```python
import functools

import jax
import jax.numpy as jnp
import numpy as np
from jax import lax
from jax.experimental import pallas as pl
from jax.experimental.pallas import tpu as pltpu
from jax.sharding import PartitionSpec as P

MESH = pl.DeviceIdType.MESH
F32 = jnp.float32
BF16 = jnp.bfloat16
N = 8192
CHIP_ORDER = (
    (1, 0), (3, 0), (0, 1), (0, 3), (1, 1), (3, 3), (1, 3), (3, 1),
    (2, 0), (0, 2), (2, 1), (1, 2), (2, 3), (3, 2), (2, 2),
)
Z_ORDER = (8, 7, 9, 6, 10, 5, 11, 4, 12, 3, 13, 2, 14, 1, 15)


def tables():
    p = np.arange(1024)
    tw1 = np.zeros((16, 1024))
    for beta in range(8):
        ang = 2 * np.pi * p * beta / N
        tw1[2 * beta] = (-1) ** beta * np.cos(ang)
        tw1[2 * beta + 1] = (-1) ** beta * np.sin(ang)
    l = np.arange(128)
    mat = np.zeros((8, 4, 2, 16, 256))
    for bp in range(8):
        idx = np.arange(64).reshape(4, 16)
        ang = 2 * np.pi * l * (8 * (idx[..., None] - 32) + bp) / 1024
        mat[bp, :, 0, :, :128] = np.cos(ang)
        mat[bp, :, 0, :, 128:] = -np.sin(ang)
        mat[bp, :, 1, :, :128] = np.sin(ang)
        mat[bp, :, 1, :, 128:] = np.cos(ang)
    k = np.arange(512)
    ang = 2 * np.pi * ((k[:, None] * k[None, :]) % 512) / 512
    cs = np.concatenate([np.cos(ang), np.sin(ang)], axis=1)
    tt = np.arange(16)
    ang = 2 * np.pi * tt[:, None] * k[None, :] / N
    sign = (1 - 2 * (k % 2)) / N
    tw2 = np.stack([np.cos(ang) * sign, np.sin(ang) * sign], axis=1).reshape(32, 512)
    return (
        jnp.asarray(tw1, F32),
        jnp.asarray(mat.reshape(8, 128, 256), BF16),
        jnp.asarray(cs, BF16),
        jnp.asarray(tw2, F32),
    )


def add(a, b):
    return (a[0] + b[0], a[1] + b[1])


def sub(a, b):
    return (a[0] - b[0], a[1] - b[1])


def add_i(a, b):
    return (a[0] - b[1], a[1] + b[0])


def sub_i(a, b):
    return (a[0] + b[1], a[1] - b[0])


def dft8(x):
    r = 0.5**0.5
    a0, a1, a2, a3 = add(x[0], x[4]), sub(x[0], x[4]), add(x[2], x[6]), sub(x[2], x[6])
    o0, o1, o2, o3 = add(x[1], x[5]), sub(x[1], x[5]), add(x[3], x[7]), sub(x[3], x[7])
    even = [add(a0, a2), add_i(a1, a3), sub(a0, a2), sub_i(a1, a3)]
    odd = [add(o0, o2), add_i(o1, o3), sub(o0, o2), sub_i(o1, o3)]
    w1 = ((odd[1][0] - odd[1][1]) * r, (odd[1][0] + odd[1][1]) * r)
    w3 = ((-odd[3][0] - odd[3][1]) * r, (odd[3][0] - odd[3][1]) * r)
    return [
        add(even[0], odd[0]), add(even[1], w1), add_i(even[2], odd[2]), add(even[3], w3),
        sub(even[0], odd[0]), sub(even[1], w1), sub_i(even[2], odd[2]), sub(even[3], w3),
    ]


def image_kernel(
    part, cover, tw1_h, mat_h, cs_h, tw2_h,
    image, halo,
    xin, pair_out, pair_in, rows_out, rows_in, mid, spec, slab_out, slab_in, slab_f, z_out, z_in, acc,
    halo_out, tw1, mat, cs, tw2,
    sem_in, sem_tab, ps, pr, cs_s, cr, ss, sr, zs, zr, hs, hr,
):
    vis = lax.axis_index("vis")
    row = lax.axis_index("row")
    col = lax.axis_index("col")
    core = vis % 2
    ylo = vis // 2
    x = col % 4
    y = (col // 4) * 2 + ylo
    chip = ylo * 8 + col
    mine = core * 16 + chip
    linear = vis * 128 + row * 8 + col

    def at(v, r, c):
        return {"vis": v, "row": r, "col": c}

    def chip_of(dx, dy):
        xx, yy = (x + dx) % 4, (y + dy) % 4
        return yy % 2, (yy // 2) * 4 + xx

    def neighbour(step):
        n = (linear + step) % 512
        return at(n // 128, (n // 8) % 16, n % 8)

    partner = at(vis + 1 - 2 * core, row, col)
    chips = [chip_of(dx, dy) for dx, dy in CHIP_ORDER]
    slab = [partner]
    for cy, cc in chips:
        slab.append(at(cy * 2 + core, row, cc))
        slab.append(at(cy * 2 + 1 - core, row, cc))
    depth = [at(vis, (row + dz) % 16, col) for dz in Z_ORDER]
    after, before = neighbour(1), neighbour(511)

    barrier = pltpu.get_barrier_semaphore()
    for peer in depth + slab + [after, before]:
        pl.semaphore_signal(barrier, inc=1, device_id=peer, device_id_type=MESH)

    def rows_of(half, blk):
        return pl.ds(pl.multiple_of(half * 256 + blk * 128, 128), 128)

    loads = []
    for h, half in enumerate((1 - core, core)):
        for blk in range(2):
            for ri in range(2):
                slot = h * 4 + blk * 2 + ri
                c = pltpu.make_async_copy(
                    part.at[ri, rows_of(half, blk)], xin.at[slot], sem_in.at[slot]
                )
                c.start()
                loads.append(c)
    tabs = [
        pltpu.make_async_copy(src, dst, sem_tab.at[i])
        for i, (src, dst) in enumerate(((tw1_h, tw1), (mat_h, mat), (cs_h, cs), (tw2_h, tw2)))
    ]
    for c in tabs:
        c.start()
    pl.semaphore_wait(barrier, len(depth) + len(slab) + 2)

    def masked(slot, half, blk, dst, dslot):
        def one(j, carry):
            lanes = pl.ds(pl.multiple_of(j * 128, 128), 128)
            m = jnp.full((128, 128), cover[half * 2 + blk, j].astype(F32)).astype(BF16)
            dst[dslot, :, lanes] = xin[slot, :, lanes] * m
            return carry

        lax.fori_loop(0, 8, one, 0)

    sends = []
    for blk in range(2):
        for ri in range(2):
            slot = blk * 2 + ri
            loads[slot].wait()
            masked(slot, 1 - core, blk, pair_out, slot)
            c = pltpu.make_async_remote_copy(
                src_ref=pair_out.at[slot],
                dst_ref=pair_in.at[slot],
                send_sem=ps.at[slot],
                recv_sem=pr.at[slot],
                device_id=partner,
                device_id_type=MESH,
            )
            c.start()
            sends.append(c)
    for blk in range(2):
        for ri in range(2):
            slot = blk * 2 + ri
            loads[4 + slot].wait()
            masked(4 + slot, core, blk, xin, 4 + slot)
    for blk in range(2):
        for ri in range(2):
            slot = blk * 2 + ri
            sends[slot].wait_recv()

            def one(i, carry):
                r = pl.ds(pl.multiple_of(i * 16, 16), 16)
                s = xin[4 + slot, r, :].astype(F32) + pair_in[slot, r, :].astype(F32)
                rows_out[blk * 8 + i, ri] = s.astype(BF16)
                return carry

            lax.fori_loop(0, 8, one, 0)

    chip_sends = []
    for i, (cy, cc) in enumerate(chips):
        c = pltpu.make_async_remote_copy(
            src_ref=rows_out.at[cy * 8 + cc],
            dst_ref=rows_in.at[chip],
            send_sem=cs_s.at[i],
            recv_sem=cr.at[i],
            device_id=at(cy * 2 + core, row, cc),
            device_id_type=MESH,
        )
        c.start()
        chip_sends.append(c)
    rows_in[chip] = rows_out[chip]
    for c in sends:
        c.wait_send()
    for c in tabs:
        c.wait()
    for c in chip_sends:
        c.wait_recv()

    def stage_one(q, carry):
        lanes = pl.ds(pl.multiple_of(q * 128, 128), 128)
        xs = []
        for c in range(8):
            xs.append(
                tuple(
                    rows_in[c, ri, :, lanes].astype(F32) + rows_in[8 + c, ri, :, lanes].astype(F32)
                    for ri in range(2)
                )
            )
        for beta, (re, im) in enumerate(dft8(xs)):
            wr = jnp.broadcast_to(tw1[2 * beta : 2 * beta + 1, lanes], (16, 128))
            wi = jnp.broadcast_to(tw1[2 * beta + 1 : 2 * beta + 2, lanes], (16, 128))
            mid[beta, q, 0] = re * wr - im * wi
            mid[beta, q, 1] = re * wi + im * wr
        return carry

    lax.fori_loop(0, 8, stage_one, 0)

    def stage_two(beta, carry):
        rows = pl.ds(pl.multiple_of(beta * 16, 16), 16)
        xs = [(mid[beta, q, 0], mid[beta, q, 1]) for q in range(8)]
        for bp, (re, im) in enumerate(dft8(xs)):
            spec[bp, rows, 0:128] = re.astype(BF16)
            spec[bp, rows, 128:256] = im.astype(BF16)
        return carry

    lax.fori_loop(0, 8, stage_two, 0)

    def stage_three(bp, carry):
        out = lax.dot_general(
            mat[bp], spec[bp], (((1,), (1,)), ((), ())), preferred_element_type=F32
        ).astype(BF16)
        for v in range(4):
            slab_out[v * 8 + bp] = out[v * 32 : (v + 1) * 32]
        return carry

    lax.fori_loop(0, 8, stage_three, 0)

    slab_sends = []
    places = []
    for cy, cc in chips:
        places.append((cy * 2 + core, cc))
        places.append((cy * 2 + 1 - core, cc))
    places.append((vis + 1 - 2 * core, col))
    for i, (v, c_) in enumerate(places):
        c = pltpu.make_async_remote_copy(
            src_ref=slab_out.at[v * 8 + c_],
            dst_ref=slab_in.at[mine],
            send_sem=ss.at[i],
            recv_sem=sr.at[i],
            device_id=at(v, row, c_),
            device_id_type=MESH,
        )
        c.start()
        slab_sends.append(c)
    slab_in[mine] = slab_out[vis * 8 + col]
    for c in chip_sends:
        c.wait_send()
    for c in slab_sends:
        c.wait_recv()

    def widen(d, carry):
        slab_f[pl.ds(pl.multiple_of(d * 32, 32), 32), :] = slab_in[d].astype(F32)
        return carry

    lax.fori_loop(0, 32, widen, 0)
    for z in range(16):
        z_out[z, :, 0:128] = slab_f[pl.ds(z, 32, stride=32), :].astype(BF16)
        z_out[z, :, 128:256] = slab_f[pl.ds(16 + z, 32, stride=32), :].astype(BF16)
    z_sends = []
    for i, dz in enumerate(Z_ORDER):
        c = pltpu.make_async_remote_copy(
            src_ref=z_out.at[(row + dz) % 16],
            dst_ref=z_in.at[row],
            send_sem=zs.at[i],
            recv_sem=zr.at[i],
            device_id=depth[i],
            device_id_type=MESH,
        )
        c.start()
        z_sends.append(c)
    z_in[row] = z_out[row]
    for c in slab_sends:
        c.wait_send()
    for c in z_sends:
        c.wait_recv()

    out = lax.dot_general(
        z_in[...].reshape(512, 256), cs[...], (((0,), (0,)), ((), ())), preferred_element_type=F32
    )
    for i in range(8):
        acc[i] = out[:, i * 128 : (i + 1) * 128]

    def last(q, carry):
        lo = pl.ds(pl.multiple_of(q * 128, 128), 128)
        vs = []
        for tt in range(16):
            top, bot = pl.ds(tt, 8, stride=16), pl.ds(128 + tt, 8, stride=16)
            re = acc[q, top, :] - acc[4 + q, bot, :]
            im = acc[4 + q, top, :] + acc[q, bot, :]
            wr = jnp.broadcast_to(tw2[2 * tt : 2 * tt + 1, lo], (8, 128))
            wi = jnp.broadcast_to(tw2[2 * tt + 1 : 2 * tt + 2, lo], (8, 128))
            vs.append((re * wr - im * wi, re * wi + im * wr))
        even = dft8([add(vs[t], vs[t + 8]) for t in range(8)])
        turned = []
        for t in range(8):
            a, b = float(np.cos(np.pi * t / 8)), float(np.sin(np.pi * t / 8))
            re, im = sub(vs[t], vs[t + 8])
            turned.append((re * a - im * b, re * b + im * a))
        odd = dft8(turned)
        for i, k in enumerate((6, 7, 0, 1)):
            image[:, pl.ds(pl.multiple_of((2 * i) * 512 + q * 128, 128), 128)] = even[k][0]
            image[:, pl.ds(pl.multiple_of((2 * i + 1) * 512 + q * 128, 128), 128)] = odd[k][0]
        return carry

    lax.fori_loop(0, 4, last, 0)

    for i in range(2):
        for j in range(4):
            lanes = slice(j * 1024, (j + 1) * 1024)
            halo_out[0, i * 4 + j : i * 4 + j + 1, :] = image[i : i + 1, lanes]
            halo_out[1, i * 4 + j : i * 4 + j + 1, :] = image[6 + i : 7 + i, lanes]
    halo_sends = []
    for i, peer in enumerate((before, after)):
        c = pltpu.make_async_remote_copy(
            src_ref=halo_out.at[i],
            dst_ref=halo.at[1 - i],
            send_sem=hs.at[i],
            recv_sem=hr.at[i],
            device_id=peer,
            device_id_type=MESH,
        )
        c.start()
        halo_sends.append(c)
    for c in z_sends:
        c.wait_send()
    for c in halo_sends:
        c.wait()


def image_rows(partials, coverage):
    any_spec = pl.BlockSpec(memory_space=pl.ANY)
    vmem = pl.BlockSpec(memory_space=pltpu.VMEM)
    dma = pltpu.SemaphoreType.DMA
    return pl.pallas_call(
        image_kernel,
        out_shape=(
            jax.ShapeDtypeStruct((8, 4096), F32),
            jax.ShapeDtypeStruct((2, 8, 1024), F32),
        ),
        in_specs=[any_spec, pl.BlockSpec(memory_space=pltpu.SMEM)] + [any_spec] * 4,
        out_specs=(vmem, vmem),
        scratch_shapes=[
            pltpu.VMEM((8, 128, 1024), BF16),
            pltpu.VMEM((4, 128, 1024), BF16),
            pltpu.VMEM((4, 128, 1024), BF16),
            pltpu.VMEM((16, 2, 16, 1024), BF16),
            pltpu.VMEM((16, 2, 16, 1024), BF16),
            pltpu.VMEM((8, 8, 2, 16, 128), F32),
            pltpu.VMEM((8, 128, 256), BF16),
            pltpu.VMEM((32, 32, 128), BF16),
            pltpu.VMEM((32, 32, 128), BF16),
            pltpu.VMEM((1024, 128), F32),
            pltpu.VMEM((16, 32, 256), BF16),
            pltpu.VMEM((16, 32, 256), BF16),
            pltpu.VMEM((8, 256, 128), F32),
            pltpu.VMEM((2, 8, 1024), F32),
            pltpu.VMEM((16, 1024), F32),
            pltpu.VMEM((8, 128, 256), BF16),
            pltpu.VMEM((512, 1024), BF16),
            pltpu.VMEM((32, 512), F32),
            dma((8,)), dma((4,)), dma((4,)), dma((4,)), dma((15,)), dma((15,)),
            dma((31,)), dma((31,)), dma((15,)), dma((15,)), dma((2,)), dma((2,)),
        ],
        name="image_rows",
        compiler_params=pltpu.CompilerParams(
            collective_id=0, has_side_effects=True, vmem_limit_bytes=40 * 2**20
        ),
    )(partials, coverage, *tables())


def conv_kernel(chunk, image, halo, w1, w2, b2, out, ext, shifted):
    ext[2:10, :] = image[...]
    for i in range(2):
        for j in range(4):
            lanes = slice(j * 1024, (j + 1) * 1024)
            ext[i : i + 1, lanes] = halo[0, i * 4 + j : i * 4 + j + 1, :]
            ext[10 + i : 11 + i, lanes] = halo[1, i * 4 + j : i * 4 + j + 1, :]
    width = image.shape[1]
    ext[12:16, :] = jnp.ones((4, width), F32)
    full = ext[...]
    lane = lax.broadcasted_iota(jnp.int32, full.shape, 1)
    for i, delta in enumerate(range(-2, 3)):
        if delta == 0:
            v = full
        else:
            v = pltpu.roll(full, (-delta) % width, 1)
            inside = (lane + delta >= 0) & (lane + delta < width)
            v = jnp.where(inside, v, 0.0)
        hi = v.astype(BF16)
        lo = (v - hi.astype(F32)).astype(BF16)
        shifted[i * 48 : i * 48 + 16, :] = hi
        shifted[i * 48 + 16 : i * 48 + 32, :] = lo
        shifted[i * 48 + 32 : i * 48 + 48, :] = hi

    def one(c, carry):
        lanes = pl.ds(pl.multiple_of(c * chunk, chunk), chunk)
        at = c * chunk + lax.broadcasted_iota(jnp.int32, (320, 128), 1)
        parts = []
        for s in range(3):
            h = jnp.dot(w1[...], shifted[s * 48 : s * 48 + 144, lanes], preferred_element_type=F32)
            h = jnp.maximum(h, 0.0)
            if s == 0:
                edge = jnp.where(at > 0, h[:, :128], 0.0)
                h = jnp.concatenate([edge, h[:, 128:]], axis=1)
            if s == 2:
                edge = jnp.where(at + (chunk - 128) < width - 1, h[:, chunk - 128 :], 0.0)
                h = jnp.concatenate([h[:, : chunk - 128], edge], axis=1)
            parts.append(h.astype(BF16))
        hidden = jnp.concatenate(parts, axis=0)
        o = jnp.dot(w2[...], hidden, preferred_element_type=F32) + b2[...]
        out[:, :, lanes] = o.reshape(32, 8, chunk).astype(BF16)
        return carry

    lax.fori_loop(0, width // chunk, one, 0)


def conv_weights(conv_one, bias_one, conv_two, bias_two):
    linear = lax.axis_index("vis") * 128 + lax.axis_index("row") * 8 + lax.axis_index("col")
    hr = jnp.arange(10)
    ir = jnp.arange(16)
    tap = (ir[None, :, None] == hr[:, None, None] + jnp.arange(3)[None, None, :]).astype(F32)
    w1 = jnp.einsum("hir,krs->hksi", tap, conv_one, precision=lax.Precision.HIGHEST)
    ones_row = ((ir[None, :] == 12) & (jnp.arange(3)[:, None] == 1)).astype(F32)
    w1 = w1 + bias_one[None, :, None, None] * ones_row[None, None]
    keep = ~(((hr == 0) & (linear == 0)) | ((hr == 9) & (linear == 511)))
    seen = ~(((ir < 2) & (linear == 0)) | ((ir // 2 == 5) & (linear == 511)))
    w1 = w1 * (keep[:, None] & seen[None, :]).astype(F32)[:, None, None, :]
    hi = w1.astype(BF16)
    lo = (w1 - hi.astype(F32)).astype(BF16)
    w1 = jnp.stack([hi, hi, lo], axis=3).reshape(320, 144)
    b = jnp.arange(8)
    tap2 = (hr[None, :, None] == b[:, None, None] + jnp.arange(3)[None, None, :]).astype(BF16)
    w2 = jnp.einsum("bhr,rskj->kbshj", tap2, conv_two, preferred_element_type=F32)
    w2 = w2.astype(BF16).reshape(256, 960)
    b2 = jnp.repeat(bias_two, 8)[:, None]
    return w1, w2, b2


def convolve(image, halo, conv_one, bias_one, conv_two, bias_two):
    chunk = 512
    w1, w2, b2 = conv_weights(conv_one, bias_one, conv_two, bias_two)
    vmem = pl.BlockSpec(memory_space=pltpu.VMEM)
    return pl.pallas_call(
        functools.partial(conv_kernel, chunk),
        out_shape=jax.ShapeDtypeStruct((32, 8, 4096), BF16),
        in_specs=[vmem] * 5,
        out_specs=vmem,
        scratch_shapes=[pltpu.VMEM((16, 4096), F32), pltpu.VMEM((240, 4096), BF16)],
        name="convolve",
        compiler_params=pltpu.CompilerParams(vmem_limit_bytes=40 * 2**20),
    )(image, halo, w1, w2, b2)


def local(partials, coverage, conv_one, bias_one, conv_two, bias_two):
    image, halo = image_rows(partials[0], coverage[0])
    return convolve(image, halo, conv_one, bias_one, conv_two, bias_two)


def solution(mesh):
    placed = (P("vis", None, "row", "col"), P("vis", "row", "col"), P(), P(), P(), P())
    return jax.shard_map(
        local,
        mesh=mesh,
        in_specs=placed,
        out_specs=P(None, ("vis", "row", "col"), None),
        check_vma=False,
    )
```

```python
import functools

import jax
import jax.numpy as jnp
import numpy as np
from jax import lax
from jax.experimental import pallas as pl
from jax.experimental.pallas import tpu as pltpu
from jax.sharding import PartitionSpec as P

MESH = pl.DeviceIdType.MESH
F32 = jnp.float32
BF16 = jnp.bfloat16
N = 8192
VMEM_LIMIT = 61 * 2**20
CHIP_ORDER = (
    (1, 0), (3, 0), (0, 1), (0, 3), (1, 1), (3, 3), (1, 3), (3, 1),
    (2, 0), (0, 2), (2, 1), (1, 2), (2, 3), (3, 2), (2, 2),
)
Z_ORDER = (8, 7, 9, 6, 10, 5, 11, 4, 12, 3, 13, 2, 14, 1, 15)


def tables():
    p = np.arange(1024)
    tw1 = np.zeros((16, 1024))
    for beta in range(8):
        ang = 2 * np.pi * p * beta / N
        tw1[2 * beta] = (-1) ** beta * np.cos(ang)
        tw1[2 * beta + 1] = (-1) ** beta * np.sin(ang)
    l = np.arange(128)
    mat = np.zeros((8, 64, 256))
    for bp in range(8):
        ang = 2 * np.pi * l * (8 * (np.arange(64)[:, None] - 32) + bp) / 1024
        mat[bp, :, :128] = np.cos(ang)
        mat[bp, :, 128:] = -np.sin(ang)
    k = np.arange(512)
    ang = 2 * np.pi * ((k[:, None] * k[None, :]) % 512) / 512
    cs = np.concatenate([np.cos(ang), np.sin(ang)], axis=1)
    tt = np.arange(16)
    ang = 2 * np.pi * tt[:, None] * k[None, :] / N
    sign = (1 - 2 * (k % 2)) / N
    tw2 = np.stack([np.cos(ang) * sign, np.sin(ang) * sign], axis=1).reshape(32, 512)
    return (
        jnp.asarray(tw1, F32),
        jnp.asarray(mat, BF16),
        jnp.asarray(cs, BF16),
        jnp.asarray(tw2, F32),
    )


def add(a, b):
    return (a[0] + b[0], a[1] + b[1])


def sub(a, b):
    return (a[0] - b[0], a[1] - b[1])


def add_i(a, b):
    return (a[0] - b[1], a[1] + b[0])


def sub_i(a, b):
    return (a[0] + b[1], a[1] - b[0])


def dft8(x):
    r = 0.5**0.5
    a0, a1, a2, a3 = add(x[0], x[4]), sub(x[0], x[4]), add(x[2], x[6]), sub(x[2], x[6])
    o0, o1, o2, o3 = add(x[1], x[5]), sub(x[1], x[5]), add(x[3], x[7]), sub(x[3], x[7])
    even = [add(a0, a2), add_i(a1, a3), sub(a0, a2), sub_i(a1, a3)]
    odd = [add(o0, o2), add_i(o1, o3), sub(o0, o2), sub_i(o1, o3)]
    w1 = ((odd[1][0] - odd[1][1]) * r, (odd[1][0] + odd[1][1]) * r)
    w3 = ((-odd[3][0] - odd[3][1]) * r, (odd[3][0] - odd[3][1]) * r)
    return [
        add(even[0], odd[0]), add(even[1], w1), add_i(even[2], odd[2]), add(even[3], w3),
        sub(even[0], odd[0]), sub(even[1], w1), sub_i(even[2], odd[2]), sub(even[3], w3),
    ]


def build_weights(linear, small, conv_two, w1, w2, base, wide):
    first = (linear == 0).astype(F32)
    final = (linear == 511).astype(F32)
    lane = lax.broadcasted_iota(jnp.int32, (32, 256), 1)
    taps = jnp.zeros((32, 256), F32)
    for r in range(3):
        for s in range(3):
            i = r * 3 + s
            taps = jnp.where(lane == s * 48 + r, small[:, i : i + 1], taps)

    def split(v):
        hi = v.astype(BF16).astype(F32)
        return hi, v - hi

    hi, lo = split(taps)
    taps = hi + pltpu.roll(hi, 16, 1) + pltpu.roll(lo, 32, 1)
    hi, lo = split(small[:, 9:10])
    shift = jnp.where(lane == 60, hi, 0.0) + jnp.where(lane == 92, lo, 0.0)
    place = lane % 16
    seen = 1.0 - first * (place < 2).astype(F32)
    seen = seen - final * ((place == 10) | (place == 11)).astype(F32)
    for hr in range(10):
        block = (pltpu.roll(taps, hr, 1) if hr else taps) + shift
        block = block * seen
        if hr == 0:
            block = block * (1.0 - first)
        if hr == 9:
            block = block * (1.0 - final)
        w1[hr * 32 : (hr + 1) * 32, :] = block[:, :144].astype(BF16)
    base[...] = jnp.zeros((32, 1024), F32)
    for r in range(3):
        for s in range(3):
            at = s * 320 + r * 32
            base[:, at : at + 32] = conv_two[r, s].astype(F32)
    hi, lo = split(small[:, 10:11])
    lane = lax.broadcasted_iota(jnp.int32, (32, 128), 1)
    offset = jnp.where(lane == 64, hi, 0.0) + jnp.where(lane == 65, lo, 0.0)
    for b in range(8):
        block = pltpu.roll(base[...], b * 32, 1) if b else base[...]
        for i in range(8):
            piece = block[:, i * 128 : (i + 1) * 128]
            if i == 7:
                piece = piece + offset
            wide[i, pl.ds(b, 32, stride=8), :] = piece
    for i in range(8):
        w2[:, i * 128 : (i + 1) * 128] = wide[i].astype(BF16)


def image_kernel(
    part, cover, tw1_h, mat_h, cs_h, tw2_h, small, conv_two,
    image, halo, w1, w2,
    xin, pair_out, pair_in, rows_out, rows_in, mid, spec, slab_out, slab_in, slab_f, z_out, z_in, acc,
    halo_out, tw1, mat, cs, tw2, base, wide,
    sem_in, sem_tab, ps, pr, cs_s, cr, ss, sr, zs, zr, hs, hr, near,
):
    vis = lax.axis_index("vis")
    row = lax.axis_index("row")
    col = lax.axis_index("col")
    core = vis % 2
    ylo = vis // 2
    x = col % 4
    y = (col // 4) * 2 + ylo
    chip = ylo * 8 + col
    mine = core * 16 + chip
    linear = vis * 128 + row * 8 + col

    def at(v, r, c):
        return {"vis": v, "row": r, "col": c}

    def chip_of(dx, dy):
        xx, yy = (x + dx) % 4, (y + dy) % 4
        return yy % 2, (yy // 2) * 4 + xx

    def neighbour(step):
        n = (linear + step) % 512
        return at(n // 128, (n // 8) % 16, n % 8)

    def along(dz):
        return at(vis, (row + dz) % 16, col)

    def send(src, dst, send_sem, recv_sem, peer):
        c = pltpu.make_async_remote_copy(
            src_ref=src, dst_ref=dst, send_sem=send_sem, recv_sem=recv_sem,
            device_id=peer, device_id_type=MESH,
        )
        c.start()
        return c

    def spread_word(level):
        for dz in (2**level, 16 - 2**level):
            pl.semaphore_signal(near.at[level], inc=1, device_id=along(dz), device_id_type=MESH)

    partner = at(vis + 1 - 2 * core, row, col)
    chips = [chip_of(dx, dy) for dx, dy in CHIP_ORDER]
    slab = [partner]
    for cy, cc in chips:
        slab.append(at(cy * 2 + core, row, cc))
        slab.append(at(cy * 2 + 1 - core, row, cc))
    after, before = neighbour(1), neighbour(511)

    barrier = pltpu.get_barrier_semaphore()
    greeted = [along(1), along(15), after, before] + slab
    for peer in greeted:
        pl.semaphore_signal(barrier, inc=1, device_id=peer, device_id_type=MESH)

    def rows_of(half, blk):
        return pl.ds(pl.multiple_of(half * 256 + blk * 128, 128), 128)

    loads = []
    for h, half in enumerate((1 - core, core)):
        for blk in range(2):
            for ri in range(2):
                slot = h * 4 + blk * 2 + ri
                c = pltpu.make_async_copy(
                    part.at[ri, rows_of(half, blk)], xin.at[slot], sem_in.at[slot]
                )
                c.start()
                loads.append(c)
    tabs = [
        pltpu.make_async_copy(src, dst, sem_tab.at[i])
        for i, (src, dst) in enumerate(((tw1_h, tw1), (mat_h, mat), (cs_h, cs), (tw2_h, tw2)))
    ]
    for c in tabs:
        c.start()

    def masked(slot, half, blk, dst, dslot):
        def one(j, carry):
            lanes = pl.ds(pl.multiple_of(j * 128, 128), 128)
            m = jnp.full((128, 128), cover[half * 2 + blk, j].astype(F32)).astype(BF16)
            dst[dslot, :, lanes] = xin[slot, :, lanes] * m
            return carry

        lax.fori_loop(0, 8, one, 0)

    for blk in range(2):
        for ri in range(2):
            slot = blk * 2 + ri
            loads[slot].wait()
            masked(slot, 1 - core, blk, pair_out, slot)
    pl.semaphore_wait(barrier, len(greeted))
    spread_word(0)
    sends = [
        send(pair_out.at[slot], pair_in.at[slot], ps.at[slot], pr.at[slot], partner)
        for slot in range(4)
    ]
    for blk in range(2):
        for ri in range(2):
            slot = blk * 2 + ri
            loads[4 + slot].wait()
            masked(4 + slot, core, blk, xin, 4 + slot)
    for blk in range(2):
        a, b = blk * 2, blk * 2 + 1
        sends[a].wait_recv()
        sends[b].wait_recv()

        def one(i, carry):
            r = pl.ds(pl.multiple_of(i * 16, 16), 16)
            re = xin[4 + a, r, :].astype(F32) + pair_in[a, r, :].astype(F32)
            im = xin[4 + b, r, :].astype(F32) + pair_in[b, r, :].astype(F32)
            rows_out[0, blk * 8 + i] = jnp.concatenate([re[:8], im[:8]], axis=0).astype(BF16)
            rows_out[1, blk * 8 + i] = jnp.concatenate([re[8:], im[8:]], axis=0).astype(BF16)
            return carry

        lax.fori_loop(0, 8, one, 0)

    chip_sends = []
    for h in range(2):
        batch = []
        for i, (cy, cc) in enumerate(chips):
            peer = at(cy * 2 + core, row, cc)
            src, dst = rows_out.at[h, cy * 8 + cc], rows_in.at[h, chip]
            batch.append(send(src, dst, cs_s.at[h * 15 + i], cr.at[h * 15 + i], peer))
        chip_sends.append(batch)
    for h in range(2):
        rows_in[h, chip] = rows_out[h, chip]
    pl.semaphore_wait(near.at[0], 2)
    spread_word(1)
    build_weights(linear, small, conv_two, w1, w2, base, wide)
    pl.semaphore_wait(near.at[1], 2)
    spread_word(2)
    for c in tabs:
        c.wait()

    places = []
    for cy, cc in chips:
        places.append((cy * 2 + core, cc))
        places.append((cy * 2 + 1 - core, cc))
    places.append((vis + 1 - 2 * core, col))

    def transform(h):
        def stage_one(q, carry):
            lanes = pl.ds(pl.multiple_of(q * 128, 128), 128)
            xs = []
            for c in range(8):
                v = rows_in[h, c, :, lanes].astype(F32) + rows_in[h, 8 + c, :, lanes].astype(F32)
                xs.append((v[:8], v[8:]))
            for beta, (re, im) in enumerate(dft8(xs)):
                wr = jnp.broadcast_to(tw1[2 * beta : 2 * beta + 1, lanes], (8, 128))
                wi = jnp.broadcast_to(tw1[2 * beta + 1 : 2 * beta + 2, lanes], (8, 128))
                mid[beta, q, 0] = re * wr - im * wi
                mid[beta, q, 1] = re * wi + im * wr
            return carry

        lax.fori_loop(0, 8, stage_one, 0)

        def stage_two(g, carry):
            low = dft8([(mid[2 * g, q, 0], mid[2 * g, q, 1]) for q in range(8)])
            high = dft8([(mid[2 * g + 1, q, 0], mid[2 * g + 1, q, 1]) for q in range(8)])
            top = pl.ds(pl.multiple_of(g * 16, 16), 16)
            bot = pl.ds(pl.multiple_of(64 + g * 16, 16), 16)
            for bp in range(8):
                re = jnp.concatenate([low[bp][0], high[bp][0]], axis=0)
                im = jnp.concatenate([low[bp][1], high[bp][1]], axis=0)
                spec[bp, top, 0:128] = re.astype(BF16)
                spec[bp, top, 128:256] = im.astype(BF16)
                spec[bp, bot, 0:128] = im.astype(BF16)
                spec[bp, bot, 128:256] = (-re).astype(BF16)
            return carry

        lax.fori_loop(0, 4, stage_two, 0)

        def stage_three(bp, carry):
            out = lax.dot_general(
                mat[bp], spec[bp], (((1,), (1,)), ((), ())), preferred_element_type=F32
            ).astype(BF16)
            for v in range(4):
                slab_out[h, v * 8 + bp] = out[v * 16 : (v + 1) * 16]
            return carry

        lax.fori_loop(0, 8, stage_three, 0)
        batch = []
        for i, (v, c_) in enumerate(places):
            src, dst = slab_out.at[h, v * 8 + c_], slab_in.at[h, mine]
            batch.append(send(src, dst, ss.at[h * 31 + i], sr.at[h * 31 + i], at(v, row, c_)))
        slab_in[h, mine] = slab_out[h, vis * 8 + col]
        return batch

    def forward(h):
        def widen(d, carry):
            slab_f[pl.ds(pl.multiple_of(d * 16, 16), 16), :] = slab_in[h, d].astype(F32)
            return carry

        lax.fori_loop(0, 32, widen, 0)
        for z in range(16):
            z_out[h, z] = slab_f[pl.ds(z, 32, stride=16), :].astype(BF16)
        batch = []
        for i, dz in enumerate(Z_ORDER):
            src, dst = z_out.at[h, (row + dz) % 16], z_in.at[h, row]
            batch.append(send(src, dst, zs.at[h * 15 + i], zr.at[h * 15 + i], along(dz)))
        z_in[h, row] = z_out[h, row]
        return batch

    def collect(h):
        out = lax.dot_general(
            z_in[h].reshape(512, 128), cs[...], (((0,), (0,)), ((), ())),
            preferred_element_type=F32,
        )
        for i in range(8):
            acc[h, i] = out[:, i * 128 : (i + 1) * 128]

    slab_sends, z_sends = [], []
    for h in range(2):
        for c in chip_sends[h]:
            c.wait_recv()
        slab_sends.append(transform(h))
        for c in slab_sends[h]:
            c.wait_recv()
        if h == 0:
            pl.semaphore_wait(near.at[2], 2)
        z_sends.append(forward(h))
    for h in range(2):
        for c in z_sends[h]:
            c.wait_recv()
        collect(h)

    def last(q, carry):
        lo = pl.ds(pl.multiple_of(q * 128, 128), 128)
        vs = []
        for tt in range(16):
            h, t = tt // 8, tt % 8
            top, bot = pl.ds(t, 8, stride=8), pl.ds(64 + t, 8, stride=8)
            re = acc[h, q, top, :] - acc[h, 4 + q, bot, :]
            im = acc[h, 4 + q, top, :] + acc[h, q, bot, :]
            wr = jnp.broadcast_to(tw2[2 * tt : 2 * tt + 1, lo], (8, 128))
            wi = jnp.broadcast_to(tw2[2 * tt + 1 : 2 * tt + 2, lo], (8, 128))
            vs.append((re * wr - im * wi, re * wi + im * wr))
        even = dft8([add(vs[t], vs[t + 8]) for t in range(8)])
        turned = []
        for t in range(8):
            a, b = float(np.cos(np.pi * t / 8)), float(np.sin(np.pi * t / 8))
            re, im = sub(vs[t], vs[t + 8])
            turned.append((re * a - im * b, re * b + im * a))
        odd = dft8(turned)
        for i, k in enumerate((6, 7, 0, 1)):
            image[:, pl.ds(pl.multiple_of((2 * i) * 512 + q * 128, 128), 128)] = even[k][0]
            image[:, pl.ds(pl.multiple_of((2 * i + 1) * 512 + q * 128, 128), 128)] = odd[k][0]
        return carry

    lax.fori_loop(0, 4, last, 0)

    for i in range(2):
        for j in range(4):
            lanes = slice(j * 1024, (j + 1) * 1024)
            halo_out[0, i * 4 + j : i * 4 + j + 1, :] = image[i : i + 1, lanes]
            halo_out[1, i * 4 + j : i * 4 + j + 1, :] = image[6 + i : 7 + i, lanes]
    halo_sends = [
        send(halo_out.at[i], halo.at[1 - i], hs.at[i], hr.at[i], peer)
        for i, peer in enumerate((before, after))
    ]
    for batch in [sends] + chip_sends + slab_sends + z_sends:
        for c in batch:
            c.wait_send()
    for c in halo_sends:
        c.wait()


def image_rows(partials, coverage, small, conv_two):
    any_spec = pl.BlockSpec(memory_space=pl.ANY)
    vmem = pl.BlockSpec(memory_space=pltpu.VMEM)
    dma = pltpu.SemaphoreType.DMA
    return pl.pallas_call(
        image_kernel,
        out_shape=(
            jax.ShapeDtypeStruct((8, 4096), F32),
            jax.ShapeDtypeStruct((2, 8, 1024), F32),
            jax.ShapeDtypeStruct((320, 144), BF16),
            jax.ShapeDtypeStruct((256, 1024), BF16),
        ),
        in_specs=[any_spec, pl.BlockSpec(memory_space=pltpu.SMEM)] + [any_spec] * 4 + [vmem] * 2,
        out_specs=(vmem,) * 4,
        scratch_shapes=[
            pltpu.VMEM((8, 128, 1024), BF16),
            pltpu.VMEM((4, 128, 1024), BF16),
            pltpu.VMEM((4, 128, 1024), BF16),
            pltpu.VMEM((2, 16, 16, 1024), BF16),
            pltpu.VMEM((2, 16, 16, 1024), BF16),
            pltpu.VMEM((8, 8, 2, 8, 128), F32),
            pltpu.VMEM((8, 128, 256), BF16),
            pltpu.VMEM((2, 32, 16, 128), BF16),
            pltpu.VMEM((2, 32, 16, 128), BF16),
            pltpu.VMEM((512, 128), F32),
            pltpu.VMEM((2, 16, 32, 128), BF16),
            pltpu.VMEM((2, 16, 32, 128), BF16),
            pltpu.VMEM((2, 8, 128, 128), F32),
            pltpu.VMEM((2, 8, 1024), F32),
            pltpu.VMEM((16, 1024), F32),
            pltpu.VMEM((8, 64, 256), BF16),
            pltpu.VMEM((512, 1024), BF16),
            pltpu.VMEM((32, 512), F32),
            pltpu.VMEM((32, 1024), F32),
            pltpu.VMEM((8, 256, 128), F32),
            dma((8,)), dma((4,)), dma((4,)), dma((4,)), dma((30,)), dma((30,)),
            dma((62,)), dma((62,)), dma((30,)), dma((30,)), dma((2,)), dma((2,)),
            pltpu.SemaphoreType.REGULAR((3,)),
        ],
        name="image_rows",
        compiler_params=pltpu.CompilerParams(
            collective_id=0, has_side_effects=True, vmem_limit_bytes=VMEM_LIMIT
        ),
    )(partials, coverage, *tables(), small, conv_two)


def conv_kernel(chunk, image, halo, w1, w2, out, ext, shifted):
    width = image.shape[1]
    step = pl.program_id(0)

    @pl.when(step == 0)
    def _():
        ext[2:10, :] = image[...]
        for i in range(2):
            for j in range(4):
                lanes = slice(j * 1024, (j + 1) * 1024)
                ext[i : i + 1, lanes] = halo[0, i * 4 + j : i * 4 + j + 1, :]
                ext[10 + i : 11 + i, lanes] = halo[1, i * 4 + j : i * 4 + j + 1, :]
        ext[12:16, :] = jnp.ones((4, width), F32)
        full = ext[...]
        lane = lax.broadcasted_iota(jnp.int32, full.shape, 1)
        for i, delta in enumerate(range(-2, 3)):
            v = full
            if delta:
                inside = (lane + delta >= 0) & (lane + delta < width)
                v = jnp.where(inside, pltpu.roll(full, (-delta) % width, 1), 0.0)
            hi = v.astype(BF16)
            lo = (v - hi.astype(F32)).astype(BF16)
            shifted[i * 48 : i * 48 + 16, :] = hi
            shifted[i * 48 + 16 : i * 48 + 32, :] = lo
            shifted[i * 48 + 32 : i * 48 + 48, :] = hi

    lanes = pl.ds(pl.multiple_of(step * chunk, chunk), chunk)
    place = step * chunk + lax.broadcasted_iota(jnp.int32, (320, 128), 1)
    parts = []
    for s in range(3):
        h = jnp.dot(w1[...], shifted[s * 48 : s * 48 + 144, lanes], preferred_element_type=F32)
        h = jnp.maximum(h, 0.0)
        if s == 0:
            edge = jnp.where(place > 0, h[:, :128], 0.0)
            h = jnp.concatenate([edge, h[:, 128:]], axis=1)
        if s == 2:
            edge = jnp.where(place + (chunk - 128) < width - 1, h[:, chunk - 128 :], 0.0)
            h = jnp.concatenate([h[:, : chunk - 128], edge], axis=1)
        parts.append(h.astype(BF16))
    parts.append(jnp.ones((64, chunk), BF16))
    hidden = jnp.concatenate(parts, axis=0)
    o = jnp.dot(w2[...], hidden, preferred_element_type=F32)
    out[...] = o.reshape(32, 8, chunk).astype(BF16)


def convolve(image, halo, w1, w2):
    chunk = 512
    vmem = pl.BlockSpec(memory_space=pltpu.VMEM)
    return pl.pallas_call(
        functools.partial(conv_kernel, chunk),
        grid=(4096 // chunk,),
        out_shape=jax.ShapeDtypeStruct((32, 8, 4096), BF16),
        in_specs=[vmem] * 4,
        out_specs=pl.BlockSpec((32, 8, chunk), lambda c: (0, 0, c)),
        scratch_shapes=[pltpu.VMEM((16, 4096), F32), pltpu.VMEM((240, 4096), BF16)],
        name="convolve",
        compiler_params=pltpu.CompilerParams(vmem_limit_bytes=40 * 2**20),
    )(image, halo, w1, w2)


def local(partials, coverage, conv_one, bias_one, conv_two, bias_two):
    small = jnp.concatenate(
        [conv_one.reshape(32, 9), bias_one[:, None], bias_two[:, None]], axis=1
    )
    image, halo, w1, w2 = image_rows(partials[0], coverage[0], small, conv_two)
    return convolve(image, halo, w1, w2)


def solution(mesh):
    placed = (P("vis", None, "row", "col"), P("vis", "row", "col"), P(), P(), P(), P())
    return jax.shard_map(
        local,
        mesh=mesh,
        in_specs=placed,
        out_specs=P(None, ("vis", "row", "col"), None),
        check_vma=False,
    )
```

```python
import jax
import jax.numpy as jnp
import numpy as np
from jax import lax
from jax.experimental import pallas as pl
from jax.experimental.pallas import tpu as pltpu
from jax.sharding import PartitionSpec as P

MESH = pl.DeviceIdType.MESH
F32 = jnp.float32
BF16 = jnp.bfloat16
N = 8192
VMEM_LIMIT = 61 * 2**20
CHIP_ORDER = (
    (1, 0), (3, 0), (0, 1), (0, 3), (1, 1), (3, 3), (1, 3), (3, 1),
    (2, 0), (0, 2), (2, 1), (1, 2), (2, 3), (3, 2), (2, 2),
)
Z_ORDER = (8, 7, 9, 6, 10, 5, 11, 4, 12, 3, 13, 2, 14, 1, 15)


def tables():
    p = np.arange(1024)
    tw1 = np.zeros((16, 1024))
    for beta in range(8):
        ang = 2 * np.pi * p * beta / N
        tw1[2 * beta] = (-1) ** beta * np.cos(ang)
        tw1[2 * beta + 1] = (-1) ** beta * np.sin(ang)
    l = np.arange(128)
    mat = np.zeros((8, 64, 256))
    for bp in range(8):
        ang = 2 * np.pi * l * (8 * (np.arange(64)[:, None] - 32) + bp) / 1024
        mat[bp, :, :128] = np.cos(ang)
        mat[bp, :, 128:] = -np.sin(ang)
    k = np.arange(512)
    ang = 2 * np.pi * ((k[:, None] * k[None, :]) % 512) / 512
    cs = np.concatenate([np.cos(ang), np.sin(ang)], axis=1)
    tt = np.arange(16)
    ang = 2 * np.pi * tt[:, None] * k[None, :] / N
    sign = (1 - 2 * (k % 2)) / N
    tw2 = np.stack([np.cos(ang) * sign, np.sin(ang) * sign], axis=1).reshape(32, 512)
    return (
        jnp.asarray(tw1, F32),
        jnp.asarray(mat, BF16),
        jnp.asarray(cs, BF16),
        jnp.asarray(tw2, F32),
    )


def add(a, b):
    return (a[0] + b[0], a[1] + b[1])


def sub(a, b):
    return (a[0] - b[0], a[1] - b[1])


def add_i(a, b):
    return (a[0] - b[1], a[1] + b[0])


def sub_i(a, b):
    return (a[0] + b[1], a[1] - b[0])


def dft8(x):
    r = 0.5**0.5
    a0, a1, a2, a3 = add(x[0], x[4]), sub(x[0], x[4]), add(x[2], x[6]), sub(x[2], x[6])
    o0, o1, o2, o3 = add(x[1], x[5]), sub(x[1], x[5]), add(x[3], x[7]), sub(x[3], x[7])
    even = [add(a0, a2), add_i(a1, a3), sub(a0, a2), sub_i(a1, a3)]
    odd = [add(o0, o2), add_i(o1, o3), sub(o0, o2), sub_i(o1, o3)]
    w1 = ((odd[1][0] - odd[1][1]) * r, (odd[1][0] + odd[1][1]) * r)
    w3 = ((-odd[3][0] - odd[3][1]) * r, (odd[3][0] - odd[3][1]) * r)
    return [
        add(even[0], odd[0]), add(even[1], w1), add_i(even[2], odd[2]), add(even[3], w3),
        sub(even[0], odd[0]), sub(even[1], w1), sub_i(even[2], odd[2]), sub(even[3], w3),
    ]


def slot_of(hr, s):
    if 2 <= hr < 8:
        return s * 192 + (hr - 2) * 32
    return 576 + s * 128 + (hr if hr < 2 else hr - 6) * 32


def build_weights(linear, one_s, bias1_s, bias2_s, conv_two, w1, w2, taps, base, wide):
    first = (linear == 0).astype(F32)
    final = (linear == 511).astype(F32)
    line = lax.broadcasted_iota(jnp.int32, (1, 256), 1)

    def fill(k, carry):
        v = jnp.zeros((1, 256), F32)
        for r in range(3):
            for s in range(3):
                v = jnp.where(line == s * 48 + r, one_s[r, s, k], v)
        v = jnp.where(line == 253, bias1_s[k], v)
        taps[pl.ds(k, 1), :] = jnp.where(line == 254, bias2_s[k], v)
        return carry

    lax.fori_loop(0, 32, fill, 0)
    lane = lax.broadcasted_iota(jnp.int32, (32, 256), 1)

    def split(v):
        hi = v.astype(BF16).astype(F32)
        return hi, v - hi

    hi, lo = split(jnp.where(lane < 144, taps[...], 0.0))
    spread = hi + pltpu.roll(hi, 16, 1) + pltpu.roll(lo, 32, 1)
    hi, lo = split(taps[:, 253:254])
    shift = jnp.where(lane == 60, hi, 0.0) + jnp.where(lane == 92, lo, 0.0)
    place = lane % 16
    seen = 1.0 - first * (place < 2).astype(F32)
    seen = seen - final * ((place == 10) | (place == 11)).astype(F32)
    for hr in range(10):
        block = (pltpu.roll(spread, hr, 1) if hr else spread) + shift
        block = block * seen
        if hr == 0:
            block = block * (1.0 - first)
        if hr == 9:
            block = block * (1.0 - final)
        for s in range(3):
            at = slot_of(hr, s)
            w1[at : at + 32, :] = (pltpu.roll(block, 48 * s, 1) if s else block).astype(BF16)
    hi, lo = split(taps[:, 254:255])
    lane = lax.broadcasted_iota(jnp.int32, (32, 128), 1)
    offset = jnp.where(lane == 64, hi, 0.0) + jnp.where(lane == 65, lo, 0.0)
    for b in range(8):
        base[...] = jnp.zeros((32, 1024), F32)
        base[:, 896:1024] = offset
        for r in range(3):
            for s in range(3):
                at = slot_of(b + r, s)
                base[:, at : at + 32] = conv_two[r, s].astype(F32)
        for i in range(8):
            wide[i, pl.ds(b, 32, stride=8), :] = base[:, i * 128 : (i + 1) * 128]
    for i in range(8):
        w2[:, i * 128 : (i + 1) * 128] = wide[i].astype(BF16)


def image_kernel(
    part, cover_h, tw1_h, mat_h, cs_h, tw2_h, one_h, bias1_h, two_h, bias2_h,
    feats,
    image, halo, w1, w2, cover, one_s, bias1_s, bias2_s, conv_two, taps, ext, shifted, hidden, partial, ready,
    xin, pair_out, pair_in, rows_out, rows_in, mid, spec, slab_out, slab_in, slab_f, z_out, z_in, acc,
    halo_out, tw1, mat, cs, tw2, base, wide,
    sem_in, sem_tab, ps, pr, cs_s, cr, ss, sr, zs, zr, hs, hr, so, near,
):
    vis = lax.axis_index("vis")
    row = lax.axis_index("row")
    col = lax.axis_index("col")
    core = vis % 2
    ylo = vis // 2
    x = col % 4
    y = (col // 4) * 2 + ylo
    chip = ylo * 8 + col
    mine = core * 16 + chip
    linear = vis * 128 + row * 8 + col

    def at(v, r, c):
        return {"vis": v, "row": r, "col": c}

    def chip_of(dx, dy):
        xx, yy = (x + dx) % 4, (y + dy) % 4
        return yy % 2, (yy // 2) * 4 + xx

    def neighbour(step):
        n = (linear + step) % 512
        return at(n // 128, (n // 8) % 16, n % 8)

    def along(dz):
        return at(vis, (row + dz) % 16, col)

    def send(src, dst, send_sem, recv_sem, peer):
        c = pltpu.make_async_remote_copy(
            src_ref=src, dst_ref=dst, send_sem=send_sem, recv_sem=recv_sem,
            device_id=peer, device_id_type=MESH,
        )
        c.start()
        return c

    def spread_word(level):
        for dz in (2**level, 16 - 2**level):
            pl.semaphore_signal(near.at[level], inc=1, device_id=along(dz), device_id_type=MESH)

    partner = at(vis + 1 - 2 * core, row, col)
    chips = [chip_of(dx, dy) for dx, dy in CHIP_ORDER]
    slab = [partner]
    for cy, cc in chips:
        slab.append(at(cy * 2 + core, row, cc))
        slab.append(at(cy * 2 + 1 - core, row, cc))
    after, before = neighbour(1), neighbour(511)

    barrier = pltpu.get_barrier_semaphore()
    greeted = [along(1), along(15), after, before] + slab
    for peer in greeted:
        pl.semaphore_signal(barrier, inc=1, device_id=peer, device_id_type=MESH)

    def rows_of(half, blk):
        return pl.ds(pl.multiple_of(half * 256 + blk * 128, 128), 128)

    loads = []
    for h, half in enumerate((1 - core, core)):
        for blk in range(2):
            for ri in range(2):
                slot = h * 4 + blk * 2 + ri
                c = pltpu.make_async_copy(
                    part.at[ri, rows_of(half, blk)], xin.at[slot], sem_in.at[slot]
                )
                c.start()
                loads.append(c)
    tabs = [
        pltpu.make_async_copy(src, dst, sem_tab.at[i])
        for i, (src, dst) in enumerate(
            (
                (cover_h, cover), (tw1_h, tw1), (mat_h, mat), (cs_h, cs), (tw2_h, tw2),
                (one_h, one_s), (bias1_h, bias1_s), (two_h, conv_two), (bias2_h, bias2_s),
            )
        )
    ]
    for c in tabs:
        c.start()
    tabs[0].wait()

    def masked(slot, half, blk, dst, dslot):
        def one(j, carry):
            lanes = pl.ds(pl.multiple_of(j * 128, 128), 128)
            m = jnp.full((128, 128), cover[half * 2 + blk, j].astype(F32)).astype(BF16)
            dst[dslot, :, lanes] = xin[slot, :, lanes] * m
            return carry

        lax.fori_loop(0, 8, one, 0)

    for blk in range(2):
        for ri in range(2):
            slot = blk * 2 + ri
            loads[slot].wait()
            masked(slot, 1 - core, blk, pair_out, slot)
    pl.semaphore_wait(barrier, len(greeted))
    spread_word(0)
    sends = [
        send(pair_out.at[slot], pair_in.at[slot], ps.at[slot], pr.at[slot], partner)
        for slot in range(4)
    ]
    for blk in range(2):
        for ri in range(2):
            slot = blk * 2 + ri
            loads[4 + slot].wait()
            masked(4 + slot, core, blk, xin, 4 + slot)
    for blk in range(2):
        a, b = blk * 2, blk * 2 + 1
        sends[a].wait_recv()
        sends[b].wait_recv()

        def one(i, carry):
            r = pl.ds(pl.multiple_of(i * 16, 16), 16)
            re = xin[4 + a, r, :].astype(F32) + pair_in[a, r, :].astype(F32)
            im = xin[4 + b, r, :].astype(F32) + pair_in[b, r, :].astype(F32)
            rows_out[0, blk * 8 + i] = jnp.concatenate([re[:8], im[:8]], axis=0).astype(BF16)
            rows_out[1, blk * 8 + i] = jnp.concatenate([re[8:], im[8:]], axis=0).astype(BF16)
            return carry

        lax.fori_loop(0, 8, one, 0)

    chip_sends = []
    for h in range(2):
        batch = []
        for i, (cy, cc) in enumerate(chips):
            peer = at(cy * 2 + core, row, cc)
            src, dst = rows_out.at[h, cy * 8 + cc], rows_in.at[h, chip]
            batch.append(send(src, dst, cs_s.at[h * 15 + i], cr.at[h * 15 + i], peer))
        chip_sends.append(batch)
    for h in range(2):
        rows_in[h, chip] = rows_out[h, chip]
    pl.semaphore_wait(near.at[0], 2)
    spread_word(1)
    for c in tabs[1:]:
        c.wait()
    build_weights(linear, one_s, bias1_s, bias2_s, conv_two, w1, w2, taps, base, wide)
    shifted[240:256, :] = jnp.zeros((16, 4096), BF16)
    hidden[960:1024, :] = jnp.ones((64, 4096), BF16)
    ext[0:2, :] = jnp.zeros((2, 4096), F32)
    ext[10:12, :] = jnp.zeros((2, 4096), F32)
    ext[12:16, :] = jnp.ones((4, 4096), F32)
    pl.semaphore_wait(near.at[1], 2)
    spread_word(2)

    places = []
    for cy, cc in chips:
        places.append((cy * 2 + core, cc))
        places.append((cy * 2 + 1 - core, cc))
    places.append((vis + 1 - 2 * core, col))

    def transform(h):
        def stage_one(q, carry):
            lanes = pl.ds(pl.multiple_of(q * 128, 128), 128)
            xs = []
            for c in range(8):
                v = rows_in[h, c, :, lanes].astype(F32) + rows_in[h, 8 + c, :, lanes].astype(F32)
                xs.append((v[:8], v[8:]))
            for beta, (re, im) in enumerate(dft8(xs)):
                wr = jnp.broadcast_to(tw1[2 * beta : 2 * beta + 1, lanes], (8, 128))
                wi = jnp.broadcast_to(tw1[2 * beta + 1 : 2 * beta + 2, lanes], (8, 128))
                mid[beta, q, 0] = re * wr - im * wi
                mid[beta, q, 1] = re * wi + im * wr
            return carry

        lax.fori_loop(0, 8, stage_one, 0)

        def stage_two(g, carry):
            low = dft8([(mid[2 * g, q, 0], mid[2 * g, q, 1]) for q in range(8)])
            high = dft8([(mid[2 * g + 1, q, 0], mid[2 * g + 1, q, 1]) for q in range(8)])
            top = pl.ds(pl.multiple_of(g * 16, 16), 16)
            bot = pl.ds(pl.multiple_of(64 + g * 16, 16), 16)
            for bp in range(8):
                re = jnp.concatenate([low[bp][0], high[bp][0]], axis=0)
                im = jnp.concatenate([low[bp][1], high[bp][1]], axis=0)
                spec[bp, top, 0:128] = re.astype(BF16)
                spec[bp, top, 128:256] = im.astype(BF16)
                spec[bp, bot, 0:128] = im.astype(BF16)
                spec[bp, bot, 128:256] = (-re).astype(BF16)
            return carry

        lax.fori_loop(0, 4, stage_two, 0)

        def stage_three(bp, carry):
            out = lax.dot_general(
                mat[bp], spec[bp], (((1,), (1,)), ((), ())), preferred_element_type=F32
            ).astype(BF16)
            for v in range(4):
                slab_out[h, v * 8 + bp] = out[v * 16 : (v + 1) * 16]
            return carry

        lax.fori_loop(0, 8, stage_three, 0)
        batch = []
        for i, (v, c_) in enumerate(places):
            src, dst = slab_out.at[h, v * 8 + c_], slab_in.at[h, mine]
            batch.append(send(src, dst, ss.at[h * 31 + i], sr.at[h * 31 + i], at(v, row, c_)))
        slab_in[h, mine] = slab_out[h, vis * 8 + col]
        return batch

    def forward(h):
        def widen(d, carry):
            slab_f[pl.ds(pl.multiple_of(d * 16, 16), 16), :] = slab_in[h, d].astype(F32)
            return carry

        lax.fori_loop(0, 32, widen, 0)
        for z in range(16):
            z_out[h, z] = slab_f[pl.ds(z, 32, stride=16), :].astype(BF16)
        batch = []
        for i, dz in enumerate(Z_ORDER):
            src, dst = z_out.at[h, (row + dz) % 16], z_in.at[h, row]
            batch.append(send(src, dst, zs.at[h * 15 + i], zr.at[h * 15 + i], along(dz)))
        z_in[h, row] = z_out[h, row]
        return batch

    def collect(h):
        out = lax.dot_general(
            z_in[h].reshape(512, 128), cs[...], (((0,), (0,)), ((), ())),
            preferred_element_type=F32,
        )
        for i in range(8):
            acc[h, i] = out[:, i * 128 : (i + 1) * 128]

    slab_sends, z_sends = [], []
    for h in range(2):
        for c in chip_sends[h]:
            c.wait_recv()
        slab_sends.append(transform(h))
        for c in slab_sends[h]:
            c.wait_recv()
        if h == 0:
            pl.semaphore_wait(near.at[2], 2)
        z_sends.append(forward(h))
    for h in range(2):
        for c in z_sends[h]:
            c.wait_recv()
        collect(h)

    def last(q, carry):
        lo = pl.ds(pl.multiple_of(q * 128, 128), 128)
        vs = []
        for tt in range(16):
            h, t = tt // 8, tt % 8
            top, bot = pl.ds(t, 8, stride=8), pl.ds(64 + t, 8, stride=8)
            re = acc[h, q, top, :] - acc[h, 4 + q, bot, :]
            im = acc[h, 4 + q, top, :] + acc[h, q, bot, :]
            wr = jnp.broadcast_to(tw2[2 * tt : 2 * tt + 1, lo], (8, 128))
            wi = jnp.broadcast_to(tw2[2 * tt + 1 : 2 * tt + 2, lo], (8, 128))
            vs.append((re * wr - im * wi, re * wi + im * wr))
        even = dft8([add(vs[t], vs[t + 8]) for t in range(8)])
        turned = []
        for t in range(8):
            a, b = float(np.cos(np.pi * t / 8)), float(np.sin(np.pi * t / 8))
            re, im = sub(vs[t], vs[t + 8])
            turned.append((re * a - im * b, re * b + im * a))
        odd = dft8(turned)
        for i, k in enumerate((6, 7, 0, 1)):
            image[:, pl.ds(pl.multiple_of((2 * i) * 512 + q * 128, 128), 128)] = even[k][0]
            image[:, pl.ds(pl.multiple_of((2 * i + 1) * 512 + q * 128, 128), 128)] = odd[k][0]
        return carry

    lax.fori_loop(0, 4, last, 0)

    for i in range(2):
        for j in range(4):
            lanes = slice(j * 1024, (j + 1) * 1024)
            halo_out[0, i * 4 + j : i * 4 + j + 1, :] = image[i : i + 1, lanes]
            halo_out[1, i * 4 + j : i * 4 + j + 1, :] = image[6 + i : 7 + i, lanes]
    halo_sends = [
        send(halo_out.at[i], halo.at[1 - i], hs.at[i], hr.at[i], peer)
        for i, peer in enumerate((before, after))
    ]
    chunk = 512
    width = 4096

    def shift_all():
        full = ext[...]
        lane = lax.broadcasted_iota(jnp.int32, full.shape, 1)
        for i, delta in enumerate(range(-2, 3)):
            v = full
            if delta:
                inside = (lane + delta >= 0) & (lane + delta < width)
                v = jnp.where(inside, pltpu.roll(full, (-delta) % width, 1), 0.0)
            hi = v.astype(BF16)
            lo = (v - hi.astype(F32)).astype(BF16)
            shifted[i * 48 : i * 48 + 16, :] = hi
            shifted[i * 48 + 16 : i * 48 + 32, :] = lo
            shifted[i * 48 + 32 : i * 48 + 48, :] = hi

    def layer_one(c, start, per):
        lanes = pl.ds(pl.multiple_of(c * chunk, chunk), chunk)
        place = c * chunk + lax.broadcasted_iota(jnp.int32, (per, 128), 1)
        h = jnp.dot(w1[start : start + 3 * per, :], shifted[:, lanes], preferred_element_type=F32)
        h = jnp.maximum(h, 0.0)
        for s in range(3):
            v = h[s * per : (s + 1) * per]
            if s == 0:
                v = jnp.concatenate([jnp.where(place > 0, v[:, :128], 0.0), v[:, 128:]], axis=1)
            if s == 2:
                far = place + (chunk - 128) < width - 1
                edge = jnp.where(far, v[:, chunk - 128 :], 0.0)
                v = jnp.concatenate([v[:, : chunk - 128], edge], axis=1)
            hidden[start + s * per : start + (s + 1) * per, lanes] = v.astype(BF16)
        return lanes

    ext[2:10, :] = image[...]
    shift_all()

    def inner(c, carry):
        lanes = layer_one(c, 0, 192)
        partial[c] = jnp.dot(w2[:, :576], hidden[:576, lanes], preferred_element_type=F32)
        return carry

    lax.fori_loop(0, width // chunk, inner, 0)
    for batch in [sends] + chip_sends + slab_sends + z_sends:
        for c in batch:
            c.wait_send()
    for c in halo_sends:
        c.wait()
    for i in range(2):
        for j in range(4):
            lanes = slice(j * 1024, (j + 1) * 1024)
            ext[i : i + 1, lanes] = halo[0, i * 4 + j : i * 4 + j + 1, :]
            ext[10 + i : 11 + i, lanes] = halo[1, i * 4 + j : i * 4 + j + 1, :]
    shift_all()

    def write(c):
        lanes = pl.ds(pl.multiple_of(c * chunk, chunk), chunk)
        return pltpu.make_async_copy(ready.at[c], feats.at[:, :, lanes], so.at[c])

    def outer(c, carry):
        lanes = layer_one(c, 576, 128)
        o = jnp.dot(w2[:, 576:], hidden[576:, lanes], preferred_element_type=F32) + partial[c]
        ready[c] = o.reshape(32, 8, chunk).astype(BF16)
        write(c).start()
        return carry

    lax.fori_loop(0, width // chunk, outer, 0)
    for c in range(width // chunk):
        write(c).wait()


def image_features(partials, coverage, conv_one, bias_one, conv_two, bias_two):
    any_spec = pl.BlockSpec(memory_space=pl.ANY)
    dma = pltpu.SemaphoreType.DMA
    return pl.pallas_call(
        image_kernel,
        out_shape=jax.ShapeDtypeStruct((32, 8, 4096), BF16),
        in_specs=[any_spec] * 10,
        out_specs=any_spec,
        scratch_shapes=[
            pltpu.VMEM((8, 4096), F32),
            pltpu.VMEM((2, 8, 1024), F32),
            pltpu.VMEM((960, 256), BF16),
            pltpu.VMEM((256, 1024), BF16),
            pltpu.SMEM((4, 8), jnp.int32),
            pltpu.SMEM((3, 3, 32), F32),
            pltpu.SMEM((32,), F32),
            pltpu.SMEM((32,), F32),
            pltpu.VMEM((3, 3, 32, 32), BF16),
            pltpu.VMEM((32, 256), F32),
            pltpu.VMEM((16, 4096), F32),
            pltpu.VMEM((256, 4096), BF16),
            pltpu.VMEM((1024, 4096), BF16),
            pltpu.VMEM((8, 256, 512), F32),
            pltpu.VMEM((8, 32, 8, 512), BF16),
            pltpu.VMEM((8, 128, 1024), BF16),
            pltpu.VMEM((4, 128, 1024), BF16),
            pltpu.VMEM((4, 128, 1024), BF16),
            pltpu.VMEM((2, 16, 16, 1024), BF16),
            pltpu.VMEM((2, 16, 16, 1024), BF16),
            pltpu.VMEM((8, 8, 2, 8, 128), F32),
            pltpu.VMEM((8, 128, 256), BF16),
            pltpu.VMEM((2, 32, 16, 128), BF16),
            pltpu.VMEM((2, 32, 16, 128), BF16),
            pltpu.VMEM((512, 128), F32),
            pltpu.VMEM((2, 16, 32, 128), BF16),
            pltpu.VMEM((2, 16, 32, 128), BF16),
            pltpu.VMEM((2, 8, 128, 128), F32),
            pltpu.VMEM((2, 8, 1024), F32),
            pltpu.VMEM((16, 1024), F32),
            pltpu.VMEM((8, 64, 256), BF16),
            pltpu.VMEM((512, 1024), BF16),
            pltpu.VMEM((32, 512), F32),
            pltpu.VMEM((32, 1024), F32),
            pltpu.VMEM((8, 256, 128), F32),
            dma((8,)), dma((9,)), dma((4,)), dma((4,)), dma((30,)), dma((30,)),
            dma((62,)), dma((62,)), dma((30,)), dma((30,)), dma((2,)), dma((2,)), dma((8,)),
            pltpu.SemaphoreType.REGULAR((3,)),
        ],
        name="image_features",
        compiler_params=pltpu.CompilerParams(
            collective_id=0, has_side_effects=True, vmem_limit_bytes=VMEM_LIMIT
        ),
    )(partials, coverage, *tables(), conv_one, bias_one, conv_two, bias_two)


def local(partials, coverage, conv_one, bias_one, conv_two, bias_two):
    taps = conv_one.transpose(1, 2, 0)
    return image_features(partials[0], coverage[0], taps, bias_one, conv_two, bias_two)


def solution(mesh):
    placed = (P("vis", None, "row", "col"), P("vis", "row", "col"), P(), P(), P(), P())
    return jax.shard_map(
        local,
        mesh=mesh,
        in_specs=placed,
        out_specs=P(None, ("vis", "row", "col"), None),
        check_vma=False,
    )
```

```python
import jax
import jax.numpy as jnp
import numpy as np
from jax import lax
from jax.experimental import pallas as pl
from jax.experimental.pallas import tpu as pltpu
from jax.sharding import PartitionSpec as P

MESH = pl.DeviceIdType.MESH
F32 = jnp.float32
BF16 = jnp.bfloat16
N = 8192
VMEM_LIMIT = 61 * 2**20
CHIP_ORDER = (
    (1, 0), (3, 0), (0, 1), (0, 3), (1, 1), (3, 3), (1, 3), (3, 1),
    (2, 0), (0, 2), (2, 1), (1, 2), (2, 3), (3, 2), (2, 2),
)
Z_ORDER = (8, 7, 9, 6, 10, 5, 11, 4, 12, 3, 13, 2, 14, 1, 15)


def tables():
    p = np.arange(1024)
    tw1 = np.zeros((16, 1024))
    for beta in range(8):
        ang = 2 * np.pi * p * beta / N
        tw1[2 * beta] = (-1) ** beta * np.cos(ang)
        tw1[2 * beta + 1] = (-1) ** beta * np.sin(ang)
    l = np.arange(128)
    mat = np.zeros((8, 64, 256))
    for bp in range(8):
        ang = 2 * np.pi * l * (8 * (np.arange(64)[:, None] - 32) + bp) / 1024
        mat[bp, :, :128] = np.cos(ang)
        mat[bp, :, 128:] = -np.sin(ang)
    k = np.arange(512)
    ang = 2 * np.pi * ((k[:, None] * k[None, :]) % 512) / 512
    cs = np.concatenate([np.cos(ang), np.sin(ang)], axis=1)
    tt = np.arange(16)
    ang = 2 * np.pi * tt[:, None] * k[None, :] / N
    sign = (1 - 2 * (k % 2)) / N
    tw2 = np.stack([np.cos(ang) * sign, np.sin(ang) * sign], axis=1).reshape(32, 512)
    return (
        jnp.asarray(tw1, F32),
        jnp.asarray(mat, BF16),
        jnp.asarray(cs, BF16),
        jnp.asarray(tw2, F32),
    )


def add(a, b):
    return (a[0] + b[0], a[1] + b[1])


def sub(a, b):
    return (a[0] - b[0], a[1] - b[1])


def add_i(a, b):
    return (a[0] - b[1], a[1] + b[0])


def sub_i(a, b):
    return (a[0] + b[1], a[1] - b[0])


def dft8(x):
    r = 0.5**0.5
    a0, a1, a2, a3 = add(x[0], x[4]), sub(x[0], x[4]), add(x[2], x[6]), sub(x[2], x[6])
    o0, o1, o2, o3 = add(x[1], x[5]), sub(x[1], x[5]), add(x[3], x[7]), sub(x[3], x[7])
    even = [add(a0, a2), add_i(a1, a3), sub(a0, a2), sub_i(a1, a3)]
    odd = [add(o0, o2), add_i(o1, o3), sub(o0, o2), sub_i(o1, o3)]
    w1 = ((odd[1][0] - odd[1][1]) * r, (odd[1][0] + odd[1][1]) * r)
    w3 = ((-odd[3][0] - odd[3][1]) * r, (odd[3][0] - odd[3][1]) * r)
    return [
        add(even[0], odd[0]), add(even[1], w1), add_i(even[2], odd[2]), add(even[3], w3),
        sub(even[0], odd[0]), sub(even[1], w1), sub_i(even[2], odd[2]), sub(even[3], w3),
    ]


def slot_of(hr, s):
    if 2 <= hr < 8:
        return s * 192 + (hr - 2) * 32
    return 576 + s * 128 + (hr if hr < 2 else hr - 6) * 32


def build_weights(linear, one_s, bias1_s, bias2_s, conv_two, w1, w2, taps, base, wide):
    first = (linear == 0).astype(F32)
    final = (linear == 511).astype(F32)
    line = lax.broadcasted_iota(jnp.int32, (1, 256), 1)

    def fill(k, carry):
        v = jnp.zeros((1, 256), F32)
        for r in range(3):
            for s in range(3):
                v = jnp.where(line == s * 48 + r, one_s[r, s, k], v)
        v = jnp.where(line == 253, bias1_s[k], v)
        taps[pl.ds(k, 1), :] = jnp.where(line == 254, bias2_s[k], v)
        return carry

    lax.fori_loop(0, 32, fill, 0)
    lane = lax.broadcasted_iota(jnp.int32, (32, 256), 1)

    def split(v):
        hi = v.astype(BF16).astype(F32)
        return hi, v - hi

    hi, lo = split(jnp.where(lane < 144, taps[...], 0.0))
    spread = hi + pltpu.roll(hi, 16, 1) + pltpu.roll(lo, 32, 1)
    hi, lo = split(taps[:, 253:254])
    shift = jnp.where(lane == 60, hi, 0.0) + jnp.where(lane == 92, lo, 0.0)
    place = lane % 16
    seen = 1.0 - first * (place < 2).astype(F32)
    seen = seen - final * ((place == 10) | (place == 11)).astype(F32)
    for hr in range(10):
        block = (pltpu.roll(spread, hr, 1) if hr else spread) + shift
        block = block * seen
        if hr == 0:
            block = block * (1.0 - first)
        if hr == 9:
            block = block * (1.0 - final)
        for s in range(3):
            at = slot_of(hr, s)
            w1[at : at + 32, :] = (pltpu.roll(block, 48 * s, 1) if s else block).astype(BF16)
    hi, lo = split(taps[:, 254:255])
    lane = lax.broadcasted_iota(jnp.int32, (32, 128), 1)
    offset = jnp.where(lane == 64, hi, 0.0) + jnp.where(lane == 65, lo, 0.0)
    for b in range(8):
        base[...] = jnp.zeros((32, 1024), F32)
        base[:, 896:1024] = offset
        for r in range(3):
            for s in range(3):
                at = slot_of(b + r, s)
                base[:, at : at + 32] = conv_two[r, s].astype(F32)
        for i in range(8):
            wide[i, pl.ds(b, 32, stride=8), :] = base[:, i * 128 : (i + 1) * 128]
    for i in range(8):
        w2[:, i * 128 : (i + 1) * 128] = wide[i].astype(BF16)


def image_kernel(
    part, cover_h, tw1_h, mat_h, cs_h, tw2_h, one_h, bias1_h, two_h, bias2_h,
    feats,
    image, halo, w1, w2, cover, one_s, bias1_s, bias2_s, conv_two, taps, ext, shifted, hidden, partial, ready,
    xin, pair_out, pair_in, rows_out, rows_in, mid, spec, slab_out, slab_in, slab_f, z_out, z_in, acc,
    halo_out, tw1, mat, cs, tw2, base, wide,
    sem_in, sem_tab, ps, pr, cs_s, cr, ss, sr, zs, zr, hs, hr, so, near,
):
    vis = lax.axis_index("vis")
    row = lax.axis_index("row")
    col = lax.axis_index("col")
    core = vis % 2
    ylo = vis // 2
    x = col % 4
    y = (col // 4) * 2 + ylo
    chip = ylo * 8 + col
    mine = core * 16 + chip
    linear = vis * 128 + row * 8 + col

    def at(v, r, c):
        return {"vis": v, "row": r, "col": c}

    def chip_of(dx, dy):
        xx, yy = (x + dx) % 4, (y + dy) % 4
        return yy % 2, (yy // 2) * 4 + xx

    def neighbour(step):
        n = (linear + step) % 512
        return at(n // 128, (n // 8) % 16, n % 8)

    def along(dz):
        return at(vis, (row + dz) % 16, col)

    def send(src, dst, send_sem, recv_sem, peer):
        c = pltpu.make_async_remote_copy(
            src_ref=src, dst_ref=dst, send_sem=send_sem, recv_sem=recv_sem,
            device_id=peer, device_id_type=MESH,
        )
        c.start()
        return c

    def spread_word(level):
        for dz in (2**level, 16 - 2**level):
            pl.semaphore_signal(near.at[level], inc=1, device_id=along(dz), device_id_type=MESH)

    partner = at(vis + 1 - 2 * core, row, col)
    chips = [chip_of(dx, dy) for dx, dy in CHIP_ORDER]
    slab = [partner]
    for cy, cc in chips:
        slab.append(at(cy * 2 + core, row, cc))
        slab.append(at(cy * 2 + 1 - core, row, cc))
    after, before = neighbour(1), neighbour(511)

    barrier = pltpu.get_barrier_semaphore()
    greeted = [along(1), along(15), after, before] + slab
    for peer in greeted:
        pl.semaphore_signal(barrier, inc=1, device_id=peer, device_id_type=MESH)

    def rows_of(half, blk):
        return pl.ds(pl.multiple_of(half * 256 + blk * 128, 128), 128)

    loads = []
    for h, half in enumerate((1 - core, core)):
        for blk in range(2):
            for ri in range(2):
                slot = h * 4 + blk * 2 + ri
                c = pltpu.make_async_copy(
                    part.at[ri, rows_of(half, blk)], xin.at[slot], sem_in.at[slot]
                )
                c.start()
                loads.append(c)
    tabs = [
        pltpu.make_async_copy(src, dst, sem_tab.at[i])
        for i, (src, dst) in enumerate(
            (
                (cover_h, cover), (tw1_h, tw1), (mat_h, mat), (cs_h, cs), (tw2_h, tw2),
                (one_h, one_s), (bias1_h, bias1_s), (two_h, conv_two), (bias2_h, bias2_s),
            )
        )
    ]
    for c in tabs:
        c.start()
    tabs[0].wait()

    def masked(slot, half, blk, dst, dslot):
        def one(j, carry):
            lanes = pl.ds(pl.multiple_of(j * 128, 128), 128)
            m = jnp.full((128, 128), cover[half * 2 + blk, j].astype(F32)).astype(BF16)
            dst[dslot, :, lanes] = xin[slot, :, lanes] * m
            return carry

        lax.fori_loop(0, 8, one, 0)

    for blk in range(2):
        for ri in range(2):
            slot = blk * 2 + ri
            loads[slot].wait()
            masked(slot, 1 - core, blk, pair_out, slot)
    pl.semaphore_wait(barrier, len(greeted))
    spread_word(0)
    sends = [
        send(pair_out.at[slot], pair_in.at[slot], ps.at[slot], pr.at[slot], partner)
        for slot in range(4)
    ]
    for blk in range(2):
        for ri in range(2):
            slot = blk * 2 + ri
            loads[4 + slot].wait()
            masked(4 + slot, core, blk, xin, 4 + slot)
    for blk in range(2):
        a, b = blk * 2, blk * 2 + 1
        sends[a].wait_recv()
        sends[b].wait_recv()

        def one(i, carry):
            r = pl.ds(pl.multiple_of(i * 16, 16), 16)
            re = xin[4 + a, r, :].astype(F32) + pair_in[a, r, :].astype(F32)
            im = xin[4 + b, r, :].astype(F32) + pair_in[b, r, :].astype(F32)
            rows_out[0, blk * 8 + i] = jnp.concatenate([re[:8], im[:8]], axis=0).astype(BF16)
            rows_out[1, blk * 8 + i] = jnp.concatenate([re[8:], im[8:]], axis=0).astype(BF16)
            return carry

        lax.fori_loop(0, 8, one, 0)

    chip_sends = []
    for h in range(2):
        batch = []
        for i, (cy, cc) in enumerate(chips):
            peer = at(cy * 2 + core, row, cc)
            src, dst = rows_out.at[h, cy * 8 + cc], rows_in.at[h, chip]
            batch.append(send(src, dst, cs_s.at[h * 15 + i], cr.at[h * 15 + i], peer))
        chip_sends.append(batch)
    for h in range(2):
        rows_in[h, chip] = rows_out[h, chip]
    pl.semaphore_wait(near.at[0], 2)
    spread_word(1)
    for c in tabs[1:]:
        c.wait()
    build_weights(linear, one_s, bias1_s, bias2_s, conv_two, w1, w2, taps, base, wide)
    shifted[240:256, :] = jnp.zeros((16, 4096), BF16)
    hidden[960:1024, :] = jnp.ones((64, 4096), BF16)
    ext[0:2, :] = jnp.zeros((2, 4096), F32)
    ext[10:12, :] = jnp.zeros((2, 4096), F32)
    ext[12:16, :] = jnp.ones((4, 4096), F32)
    pl.semaphore_wait(near.at[1], 2)
    spread_word(2)

    places = []
    for cy, cc in chips:
        places.append((cy * 2 + core, cc))
        places.append((cy * 2 + 1 - core, cc))
    places.append((vis + 1 - 2 * core, col))

    def transform(h):
        def stage_one(q, carry):
            lanes = pl.ds(pl.multiple_of(q * 128, 128), 128)
            xs = []
            for c in range(8):
                v = rows_in[h, c, :, lanes].astype(F32) + rows_in[h, 8 + c, :, lanes].astype(F32)
                xs.append((v[:8], v[8:]))
            for beta, (re, im) in enumerate(dft8(xs)):
                wr = jnp.broadcast_to(tw1[2 * beta : 2 * beta + 1, lanes], (8, 128))
                wi = jnp.broadcast_to(tw1[2 * beta + 1 : 2 * beta + 2, lanes], (8, 128))
                mid[beta, q, 0] = re * wr - im * wi
                mid[beta, q, 1] = re * wi + im * wr
            return carry

        lax.fori_loop(0, 8, stage_one, 0)

        def stage_two(g, carry):
            low = dft8([(mid[2 * g, q, 0], mid[2 * g, q, 1]) for q in range(8)])
            high = dft8([(mid[2 * g + 1, q, 0], mid[2 * g + 1, q, 1]) for q in range(8)])
            top = pl.ds(pl.multiple_of(g * 16, 16), 16)
            bot = pl.ds(pl.multiple_of(64 + g * 16, 16), 16)
            for bp in range(8):
                re = jnp.concatenate([low[bp][0], high[bp][0]], axis=0)
                im = jnp.concatenate([low[bp][1], high[bp][1]], axis=0)
                spec[bp, top, 0:128] = re.astype(BF16)
                spec[bp, top, 128:256] = im.astype(BF16)
                spec[bp, bot, 0:128] = im.astype(BF16)
                spec[bp, bot, 128:256] = (-re).astype(BF16)
            return carry

        lax.fori_loop(0, 4, stage_two, 0)

        def stage_three(bp, carry):
            out = lax.dot_general(
                mat[bp], spec[bp], (((1,), (1,)), ((), ())), preferred_element_type=F32
            ).astype(BF16)
            for v in range(4):
                slab_out[h, v * 8 + bp] = out[v * 16 : (v + 1) * 16]
            return carry

        lax.fori_loop(0, 8, stage_three, 0)
        batch = []
        for i, (v, c_) in enumerate(places):
            src, dst = slab_out.at[h, v * 8 + c_], slab_in.at[h, mine]
            batch.append(send(src, dst, ss.at[h * 31 + i], sr.at[h * 31 + i], at(v, row, c_)))
        slab_in[h, mine] = slab_out[h, vis * 8 + col]
        return batch

    def forward(h):
        def widen(d, carry):
            slab_f[pl.ds(pl.multiple_of(d * 16, 16), 16), :] = slab_in[h, d].astype(F32)
            return carry

        lax.fori_loop(0, 32, widen, 0)
        for z in range(16):
            z_out[h, z] = slab_f[pl.ds(z, 32, stride=16), :].astype(BF16)
        batch = []
        for i, dz in enumerate(Z_ORDER):
            src, dst = z_out.at[h, (row + dz) % 16], z_in.at[h, row]
            batch.append(send(src, dst, zs.at[h * 15 + i], zr.at[h * 15 + i], along(dz)))
        z_in[h, row] = z_out[h, row]
        return batch

    def collect(h):
        out = lax.dot_general(
            z_in[h].reshape(512, 128), cs[...], (((0,), (0,)), ((), ())),
            preferred_element_type=F32,
        )
        for i in range(8):
            acc[h, i] = out[:, i * 128 : (i + 1) * 128]

    slab_sends, z_sends = [], []
    for h in range(2):
        for c in chip_sends[h]:
            c.wait_recv()
        slab_sends.append(transform(h))
    pl.semaphore_wait(near.at[2], 2)
    for h in range(2):
        for c in slab_sends[h]:
            c.wait_recv()
        z_sends.append(forward(h))
    for h in range(2):
        for c in z_sends[h]:
            c.wait_recv()
        collect(h)

    def last(q, carry):
        lo = pl.ds(pl.multiple_of(q * 128, 128), 128)
        vs = []
        for tt in range(16):
            h, t = tt // 8, tt % 8
            top, bot = pl.ds(t, 8, stride=8), pl.ds(64 + t, 8, stride=8)
            re = acc[h, q, top, :] - acc[h, 4 + q, bot, :]
            im = acc[h, 4 + q, top, :] + acc[h, q, bot, :]
            wr = jnp.broadcast_to(tw2[2 * tt : 2 * tt + 1, lo], (8, 128))
            wi = jnp.broadcast_to(tw2[2 * tt + 1 : 2 * tt + 2, lo], (8, 128))
            vs.append((re * wr - im * wi, re * wi + im * wr))
        even = dft8([add(vs[t], vs[t + 8]) for t in range(8)])
        turned = []
        for t in range(8):
            a, b = float(np.cos(np.pi * t / 8)), float(np.sin(np.pi * t / 8))
            re, im = sub(vs[t], vs[t + 8])
            turned.append((re * a - im * b, re * b + im * a))
        odd = dft8(turned)
        for i, k in enumerate((6, 7, 0, 1)):
            image[:, pl.ds(pl.multiple_of((2 * i) * 512 + q * 128, 128), 128)] = even[k][0]
            image[:, pl.ds(pl.multiple_of((2 * i + 1) * 512 + q * 128, 128), 128)] = odd[k][0]
        return carry

    lax.fori_loop(0, 4, last, 0)

    for i in range(2):
        for j in range(4):
            lanes = slice(j * 1024, (j + 1) * 1024)
            halo_out[0, i * 4 + j : i * 4 + j + 1, :] = image[i : i + 1, lanes]
            halo_out[1, i * 4 + j : i * 4 + j + 1, :] = image[6 + i : 7 + i, lanes]
    halo_sends = [
        send(halo_out.at[i], halo.at[1 - i], hs.at[i], hr.at[i], peer)
        for i, peer in enumerate((before, after))
    ]
    chunk = 512
    width = 4096

    def shift_all():
        full = ext[...]
        lane = lax.broadcasted_iota(jnp.int32, full.shape, 1)
        for i, delta in enumerate(range(-2, 3)):
            v = full
            if delta:
                inside = (lane + delta >= 0) & (lane + delta < width)
                v = jnp.where(inside, pltpu.roll(full, (-delta) % width, 1), 0.0)
            hi = v.astype(BF16)
            lo = (v - hi.astype(F32)).astype(BF16)
            shifted[i * 48 : i * 48 + 16, :] = hi
            shifted[i * 48 + 16 : i * 48 + 32, :] = lo
            shifted[i * 48 + 32 : i * 48 + 48, :] = hi

    def layer_one(c, start, per):
        lanes = pl.ds(pl.multiple_of(c * chunk, chunk), chunk)
        place = c * chunk + lax.broadcasted_iota(jnp.int32, (per, 128), 1)
        h = jnp.dot(w1[start : start + 3 * per, :], shifted[:, lanes], preferred_element_type=F32)
        h = jnp.maximum(h, 0.0)
        for s in range(3):
            v = h[s * per : (s + 1) * per]
            if s == 0:
                v = jnp.concatenate([jnp.where(place > 0, v[:, :128], 0.0), v[:, 128:]], axis=1)
            if s == 2:
                far = place + (chunk - 128) < width - 1
                edge = jnp.where(far, v[:, chunk - 128 :], 0.0)
                v = jnp.concatenate([v[:, : chunk - 128], edge], axis=1)
            hidden[start + s * per : start + (s + 1) * per, lanes] = v.astype(BF16)
        return lanes

    ext[2:10, :] = image[...]
    shift_all()

    def inner(c, carry):
        lanes = layer_one(c, 0, 192)
        partial[c] = jnp.dot(w2[:, :576], hidden[:576, lanes], preferred_element_type=F32)
        return carry

    lax.fori_loop(0, width // chunk, inner, 0)
    for batch in [sends] + chip_sends + slab_sends + z_sends:
        for c in batch:
            c.wait_send()
    for c in halo_sends:
        c.wait()
    for i in range(2):
        for j in range(4):
            lanes = slice(j * 1024, (j + 1) * 1024)
            ext[i : i + 1, lanes] = halo[0, i * 4 + j : i * 4 + j + 1, :]
            ext[10 + i : 11 + i, lanes] = halo[1, i * 4 + j : i * 4 + j + 1, :]
    shift_all()

    def write(c):
        lanes = pl.ds(pl.multiple_of(c * chunk, chunk), chunk)
        return pltpu.make_async_copy(ready.at[c], feats.at[:, :, lanes], so.at[c])

    def outer(c, carry):
        lanes = layer_one(c, 576, 128)
        o = jnp.dot(w2[:, 576:], hidden[576:, lanes], preferred_element_type=F32) + partial[c]
        ready[c] = o.reshape(32, 8, chunk).astype(BF16)
        write(c).start()
        return carry

    lax.fori_loop(0, width // chunk, outer, 0)
    for c in range(width // chunk):
        write(c).wait()


def image_features(partials, coverage, conv_one, bias_one, conv_two, bias_two):
    any_spec = pl.BlockSpec(memory_space=pl.ANY)
    dma = pltpu.SemaphoreType.DMA
    return pl.pallas_call(
        image_kernel,
        out_shape=jax.ShapeDtypeStruct((32, 8, 4096), BF16),
        in_specs=[any_spec] * 10,
        out_specs=any_spec,
        scratch_shapes=[
            pltpu.VMEM((8, 4096), F32),
            pltpu.VMEM((2, 8, 1024), F32),
            pltpu.VMEM((960, 256), BF16),
            pltpu.VMEM((256, 1024), BF16),
            pltpu.SMEM((4, 8), jnp.int32),
            pltpu.SMEM((3, 3, 32), F32),
            pltpu.SMEM((32,), F32),
            pltpu.SMEM((32,), F32),
            pltpu.VMEM((3, 3, 32, 32), BF16),
            pltpu.VMEM((32, 256), F32),
            pltpu.VMEM((16, 4096), F32),
            pltpu.VMEM((256, 4096), BF16),
            pltpu.VMEM((1024, 4096), BF16),
            pltpu.VMEM((8, 256, 512), F32),
            pltpu.VMEM((8, 32, 8, 512), BF16),
            pltpu.VMEM((8, 128, 1024), BF16),
            pltpu.VMEM((4, 128, 1024), BF16),
            pltpu.VMEM((4, 128, 1024), BF16),
            pltpu.VMEM((2, 16, 16, 1024), BF16),
            pltpu.VMEM((2, 16, 16, 1024), BF16),
            pltpu.VMEM((8, 8, 2, 8, 128), F32),
            pltpu.VMEM((8, 128, 256), BF16),
            pltpu.VMEM((2, 32, 16, 128), BF16),
            pltpu.VMEM((2, 32, 16, 128), BF16),
            pltpu.VMEM((512, 128), F32),
            pltpu.VMEM((2, 16, 32, 128), BF16),
            pltpu.VMEM((2, 16, 32, 128), BF16),
            pltpu.VMEM((2, 8, 128, 128), F32),
            pltpu.VMEM((2, 8, 1024), F32),
            pltpu.VMEM((16, 1024), F32),
            pltpu.VMEM((8, 64, 256), BF16),
            pltpu.VMEM((512, 1024), BF16),
            pltpu.VMEM((32, 512), F32),
            pltpu.VMEM((32, 1024), F32),
            pltpu.VMEM((8, 256, 128), F32),
            dma((8,)), dma((9,)), dma((4,)), dma((4,)), dma((30,)), dma((30,)),
            dma((62,)), dma((62,)), dma((30,)), dma((30,)), dma((2,)), dma((2,)), dma((8,)),
            pltpu.SemaphoreType.REGULAR((3,)),
        ],
        name="image_features",
        compiler_params=pltpu.CompilerParams(
            collective_id=0, has_side_effects=True, vmem_limit_bytes=VMEM_LIMIT
        ),
    )(partials, coverage, *tables(), conv_one, bias_one, conv_two, bias_two)


def hand_over_kernel(src, dst, buf, ins, outs):
    loads = [pltpu.make_async_copy(src.at[pl.ds(i * 4, 4)], buf.at[i], ins.at[i]) for i in range(8)]
    stores = [pltpu.make_async_copy(buf.at[i], dst.at[pl.ds(i * 4, 4)], outs.at[i]) for i in range(8)]
    for c in loads:
        c.start()
    for i in range(8):
        loads[i].wait()
        stores[i].start()
    for c in stores:
        c.wait()


def hand_over(features):
    any_spec = pl.BlockSpec(memory_space=pl.ANY)
    dma = pltpu.SemaphoreType.DMA
    return pl.pallas_call(
        hand_over_kernel,
        out_shape=jax.ShapeDtypeStruct(features.shape, features.dtype),
        in_specs=[any_spec],
        out_specs=any_spec,
        scratch_shapes=[pltpu.VMEM((8, 4, 8, 4096), BF16), dma((8,)), dma((8,))],
        name="hand_over",
        compiler_params=pltpu.CompilerParams(vmem_limit_bytes=VMEM_LIMIT),
    )(features)


def local(partials, coverage, conv_one, bias_one, conv_two, bias_two):
    taps = conv_one.transpose(1, 2, 0)
    out = image_features(partials[0], coverage[0], taps, bias_one, conv_two, bias_two)
    return hand_over(out)


def solution(mesh):
    placed = (P("vis", None, "row", "col"), P("vis", "row", "col"), P(), P(), P(), P())
    return jax.shard_map(
        local,
        mesh=mesh,
        in_specs=placed,
        out_specs=P(None, ("vis", "row", "col"), None),
        check_vma=False,
    )
```
